1024 devices in a mesh: node: 128 (over y, z, core), local: 8 (over x).
Axes of the slice: x: 8, y: 8, z: 8, core: 2. Of those that a mesh axis runs over, the one named last changes fastest.
Arguments:
- tokens: bfloat16 [4096, 4096], P('node', 'local'), may hold values from -6 to 6
- node_ids: int32 [4096, 4], P('node'), may hold values from 0 to 127, all different within a row; in each aligned block of 32 rows (0 to 31, 32 to 63, ...) at most 2 rows name the same one
- mix_weights: float32 [4096, 4], P('node'), may hold values from 0.05 to 1
- w_gate: bfloat16 [128, 4096, 1024], P('node', 'local'), may hold values from -0.09375 to 0.09375
- w_up: bfloat16 [128, 4096, 1024], P('node', 'local'), may hold values from -0.09375 to 0.09375
- w_down: bfloat16 [128, 1024, 4096], P('node', None, 'local'), may hold values from -0.1875 to 0.1875
Outputs:
- mixed: bfloat16 [4096, 4096], P('node', 'local')
The draws below stay inside these ranges and needn't reach their ends.
Inputs may be any that keep to these rules, and one draw needn't show every extreme that they name: `node_ids`: each row names 4 different experts. Among the 32 tokens of one node (aligned blocks of rows), at most 2 name the same expert, and in every draw some expert is named by exactly 2 tokens of some node.
All inputs are finite; a program needn't handle non-finite values.
Results may differ from the reference program's by a relative error of at most 0.023.
Values may be sent and summed in bfloat16 or wider, within the bound.
No kernel may reach another device: no remote copies, remote signals or barrier semaphores. Data moves between devices by JAX's collectives and lax.ppermute only.
A program may use at most 32 MiB of HBM per device.

```python
import math
import jax
import jax.numpy as jnp
import numpy as np
from jax import lax

D = 4096
HID = 1024
TOP = 4
TOK_NODE = 32
EXPERTS = 128
CAP = 2
TOKENS = 4096
N_NODE = 128
N_LOCAL = 8


def level_of(key, shape, shards, smallest, top_value):
    level = 1.0
    for dim, blocks in shards:
        heights = jax.random.uniform(jax.random.fold_in(jax.random.fold_in(key, 6), dim), (blocks,), jnp.float32, smallest / len(shards), top_value / len(shards))
        level = level * jnp.repeat(jnp.exp(heights), shape[dim] // blocks).reshape((-1,) + (1,) * (len(shape) - 1 - dim))
    return level


def shared_out(own_key, own, number, rows, amount, top, limit, skew):
    order = jax.random.permutation(own_key, amount)
    packed, ordinary = portions_of(amount, rows * top, limit, skew, True), portions_of(amount, rows * top, limit, skew, False)
    places = jnp.arange(amount)

    def named(sizes, rotation):
        used = int((sizes > 0).sum())
        fixed = max(1, used // 4)
        moved = fixed + (places - fixed + rotation * (used - fixed)) % max(1, amount - fixed)
        return jnp.zeros((amount,), jnp.int32).at[order[jnp.where(places < fixed, places, moved)]].set(jnp.asarray(sizes, jnp.int32))

    sizes = jnp.where(number % 4 == 0, named(packed, number // 4), named(ordinary, number - number // 4 - 1))
    mixed = jax.random.permutation(jax.random.fold_in(own, 3), amount)
    donor, receiver = mixed[0:amount // 2 * 2:2], mixed[1:amount // 2 * 2:2]
    slack = jnp.minimum(sizes[donor] - 1, limit - sizes[receiver]) // 2
    slack = jnp.where((donor == order[0]) | (receiver == order[0]) | (sizes[receiver] == 0), 0, jnp.maximum(slack, 0))
    moved = jax.random.randint(jax.random.fold_in(own, 4), (amount // 2,), 0, 1 << 20) % (slack + 1)
    sizes = sizes.at[donor].add(-moved).at[receiver].add(moved)
    items = jnp.searchsorted(jnp.cumsum(sizes), jnp.arange(rows * top), side="right").astype(jnp.int32)
    listing = items.reshape(top, rows).T
    listing = listing[jax.random.permutation(jax.random.fold_in(own, 1), rows)]
    rotation = jax.random.randint(jax.random.fold_in(own, 2), (rows, 1), 0, top)
    return jnp.take_along_axis(listing, (jnp.arange(top)[None, :] + rotation) % top, axis=1)


def portions_of(number_of, total, bound, slope, full):
    loads = [(1 << 20) // math.isqrt(standing ** slope) + 1 for standing in range(1, number_of + 1)]
    largest = bound if full else min(bound, max(-(-total // number_of), total * loads[0] // sum(loads)))
    least = 1 if total - largest >= number_of - 1 else 0
    given, rest = [largest] + [least] * (number_of - 1), total - largest - least * (number_of - 1)
    while rest > 0:
        free = [i for i in range(1, number_of) if given[i] < largest] or [i for i in range(1, number_of) if given[i] < bound]
        mass, remaining = sum([loads[i] for i in free]), rest
        for i in free:
            addition = min(bound - given[i], max(1, remaining * loads[i] // mass), rest)
            given[i] = given[i] + addition
            rest = rest - addition
    return np.array(given)


def normal_values(rng, dims, deviation, bound, cuts=(), held_as=jnp.bfloat16):
    drawn = jax.random.normal(rng, dims, jnp.float32) * deviation
    if len(cuts) > 0:
        drawn = level_of(rng, dims, cuts, -0.22, 0.18) * drawn
    return jnp.clip(drawn, min=-bound, max=bound).astype(held_as)


def setup_inputs(seed: int = 0) -> dict:
    arg_keys = jax.random.split(jax.random.key(seed), 7)
    tokens = normal_values(arg_keys[0], (TOKENS, D), 1.0, 6.0, ((0, 128), (1, 8)))
    node_ids_keys = jax.random.split(jax.random.fold_in(arg_keys[1], 1), TOKENS // TOK_NODE)
    node_ids_turns = jax.random.permutation(jax.random.fold_in(arg_keys[1], 3), TOKENS // TOK_NODE)
    node_ids = jax.vmap(lambda own, number: shared_out(jax.random.fold_in(arg_keys[1], 2), own, number, TOK_NODE, EXPERTS, TOP, CAP, 2))(node_ids_keys, node_ids_turns).reshape((TOKENS, TOP))
    mix_weights = jnp.clip(jnp.exp(math.log(1.0) - 2.9957323 * jax.random.uniform(arg_keys[2], (TOKENS, TOP), jnp.float32) ** level_of(arg_keys[2], (TOKENS, TOP), ((0, 128),), -0.2, 0.2)), 0.05, 1.0)
    w_gate = normal_values(arg_keys[3], (EXPERTS, D, HID), D ** -0.5, 0.09375, ((0, 128), (1, 8)))
    w_up = normal_values(arg_keys[4], (EXPERTS, D, HID), D ** -0.5, 0.09375, ((0, 128), (1, 8)))
    w_down = normal_values(arg_keys[5], (EXPERTS, HID, D), HID ** -0.5, 0.1875, ((0, 128), (2, 8)))
    return {"tokens": tokens, "node_ids": node_ids, "mix_weights": mix_weights, "w_gate": w_gate, "w_up": w_up, "w_down": w_down}


def reference(tokens, node_ids, mix_weights, w_gate, w_up, w_down):
    count = TOKENS * TOP
    flat_ids = node_ids.reshape(-1)
    owners = jnp.arange(count, dtype=jnp.int32) // TOP
    flat_mix = mix_weights.reshape(-1)
    split = D // N_LOCAL
    room = N_NODE * CAP

    def slice_sum(pieces, weight):
        parts = jnp.einsum('snd,ndh->nsh', pieces, weight.reshape(N_LOCAL, split, HID).astype(jnp.float32), precision=lax.Precision.HIGHEST)
        rounded = lax.optimization_barrier(parts.astype(jnp.bfloat16))
        return jnp.sum(rounded.astype(jnp.float32), axis=0)

    def one_expert(total, expert):
        chosen = flat_ids == expert
        index = jnp.nonzero(chosen, size=room, fill_value=0)[0].astype(jnp.int32)
        valid = (jnp.arange(room, dtype=jnp.int32) < jnp.sum(chosen.astype(jnp.int32))).astype(jnp.float32)
        owner_rows = owners[index]
        rows_in = tokens[owner_rows]
        pieces = rows_in.reshape(room, N_LOCAL, split).astype(jnp.float32)
        gate = slice_sum(pieces, w_gate[expert])
        up = slice_sum(pieces, w_up[expert])
        active = (jax.nn.silu(gate) * up).astype(jnp.bfloat16)
        result = jnp.dot(active, w_down[expert], preferred_element_type=jnp.float32).astype(jnp.bfloat16)
        result = lax.optimization_barrier(result).astype(jnp.float32)
        scaled = result * (flat_mix[index] * valid)[:, None]
        return total.at[owner_rows].add(scaled), None

    start = jnp.zeros((TOKENS, D), jnp.float32)
    total, unused = lax.scan(one_expert, start, jnp.arange(EXPERTS, dtype=jnp.int32))
    return total.astype(jnp.bfloat16)
```

```python
import jax
import jax.numpy as jnp
from jax import lax
from jax.sharding import PartitionSpec as P


def body(tokens, node_ids, mix_weights, w_gate, w_up, w_down):
    row_count, feat_width = tokens.shape
    node_count = lax.axis_size("node")
    local_count = lax.axis_size("local")
    hidden = w_gate.shape[2]
    cap = 2
    slots = node_count * cap
    share = slots // local_count

    experts = jnp.arange(node_count, dtype=jnp.int32)
    match = node_ids.T[:, None, :] == experts[None, :, None]
    hit = jnp.any(match, axis=0)
    weight = jnp.sum(jnp.where(match, mix_weights.T[:, None, :], 0.0), axis=0)
    earlier = jnp.arange(row_count)[:, None] < jnp.arange(row_count)[None, :]
    rank = jnp.dot(
        hit.astype(jnp.bfloat16), earlier.astype(jnp.bfloat16), preferred_element_type=jnp.float32
    )
    picked = hit[:, None, :] & (rank[:, None, :] == jnp.arange(cap, dtype=jnp.float32)[None, :, None])
    dispatch = picked.reshape(slots, row_count).astype(jnp.bfloat16)
    combine = jnp.where(picked, weight[:, None, :], 0.0).reshape(slots, row_count)

    outbound = jnp.dot(dispatch, tokens, preferred_element_type=jnp.float32).astype(jnp.bfloat16)
    inbound = lax.all_to_all(
        outbound.reshape(node_count, cap, feat_width), "node", split_axis=0, concat_axis=0, tiled=True
    ).reshape(slots, feat_width)

    gate_part = jnp.dot(inbound, w_gate[0], preferred_element_type=jnp.float32).astype(jnp.bfloat16)
    up_part = jnp.dot(inbound, w_up[0], preferred_element_type=jnp.float32).astype(jnp.bfloat16)
    parts = jnp.concatenate([gate_part, up_part], axis=1).reshape(local_count, share, 2 * hidden)
    parts = lax.all_to_all(parts, "local", split_axis=0, concat_axis=0, tiled=True)
    total = jnp.sum(parts.astype(jnp.float32), axis=0)
    active = (jax.nn.silu(total[:, :hidden]) * total[:, hidden:]).astype(jnp.bfloat16)

    copies = jnp.broadcast_to(active[None], (local_count, share, hidden))
    rows = lax.all_to_all(copies, "local", split_axis=0, concat_axis=0, tiled=True)
    result = jnp.dot(
        rows.reshape(slots, hidden), w_down[0], preferred_element_type=jnp.float32
    ).astype(jnp.bfloat16)
    returned = lax.all_to_all(
        result.reshape(node_count, cap, feat_width), "node", split_axis=0, concat_axis=0, tiled=True
    ).reshape(slots, feat_width)
    mixed = lax.dot_general(
        combine,
        returned.astype(jnp.float32),
        (((0,), (0,)), ((), ())),
        precision=lax.Precision.HIGHEST,
    )
    return mixed.astype(jnp.bfloat16)


def solution(mesh):
    return jax.shard_map(
        body,
        mesh=mesh,
        in_specs=(
            P("node", "local"),
            P("node", None),
            P("node", None),
            P("node", "local", None),
            P("node", "local", None),
            P("node", None, "local"),
        ),
        out_specs=P("node", "local"),
        check_vma=False,
    )
```

```python
import jax
import jax.numpy as jnp
import numpy as np
from jax import lax
from jax.sharding import PartitionSpec as P

CAP = 2
CORES = 2
BOTH = ("node", "local")
FIRST = (0, 2, 5, 7)
SECOND = (1, 3, 4, 6)
TEAM = (0, 1, 0, 1, 1, 0, 1, 0)


def seat(label, core):
    return (label + core) % 8


def body(tokens, node_ids, mix_weights, w_gate, w_up, w_down):
    row_count, feat_width = tokens.shape
    node_count = lax.axis_size("node")
    local_count = lax.axis_size("local")
    hidden = w_gate.shape[2]
    chips = node_count // CORES
    slots = node_count * CAP
    half = slots // 2
    share = slots // local_count

    chip_groups = [[chip * CORES + core for chip in range(chips)] for core in range(CORES)]
    core_swap = [(node, node ^ 1) for node in range(node_count)]
    team_groups = [
        [node * local_count + seat(label, node % CORES) for label in team]
        for node in range(node_count)
        for team in (FIRST, SECOND)
    ]
    pair_swap = [
        (node * local_count + seat(label, node % CORES), node * local_count + seat(label ^ 1, node % CORES))
        for node in range(node_count)
        for label in range(local_count)
    ]
    core = lax.axis_index("node") % CORES
    team = jnp.asarray(np.array(TEAM, np.int32))[(lax.axis_index("local") + local_count - core) % local_count]

    def exchange(array, axis, groups):
        return lax.all_to_all(
            array, axis, split_axis=0, concat_axis=0, tiled=True, axis_index_groups=groups
        )

    chip_index = jnp.arange(chips, dtype=jnp.int32) * CORES
    experts = jnp.concatenate([chip_index + core, chip_index + 1 - core])
    match = node_ids.T[:, None, :] == experts[None, :, None]
    hit = jnp.any(match, axis=0)
    weight = jnp.sum(jnp.where(match, mix_weights.T[:, None, :], 0.0), axis=0)
    earlier = jnp.arange(row_count)[:, None] < jnp.arange(row_count)[None, :]
    rank = jnp.dot(
        hit.astype(jnp.bfloat16), earlier.astype(jnp.bfloat16), preferred_element_type=jnp.float32
    )
    picked = hit[:, None, :] & (rank[:, None, :] == jnp.arange(CAP, dtype=jnp.float32)[None, :, None])
    dispatch = picked.reshape(slots, row_count).astype(jnp.bfloat16)
    combine = jnp.where(picked, weight[:, None, :], 0.0).reshape(slots, row_count)

    outbound = jnp.dot(dispatch, tokens, preferred_element_type=jnp.float32).astype(jnp.bfloat16)
    theirs = lax.ppermute(outbound[half:], "node", core_swap)
    mine = outbound[:half].reshape(chips, CAP, feat_width)
    leaving = jnp.concatenate([mine, theirs.reshape(chips, CAP, feat_width)], axis=1)
    inbound = exchange(leaving, "node", chip_groups).reshape(2, half, feat_width)

    def project(rows):
        gate = jnp.dot(rows, w_gate[0], preferred_element_type=jnp.float32)
        up = jnp.dot(rows, w_up[0], preferred_element_type=jnp.float32)
        return gate, up

    first_team = team == 0
    away = jnp.where(first_team, inbound[1], inbound[0])
    kept = jnp.where(first_team, inbound[0], inbound[1])
    gate_away, up_away = project(away)
    sent = jnp.concatenate([gate_away.astype(jnp.bfloat16), up_away.astype(jnp.bfloat16)], axis=1)
    got = lax.ppermute(sent, BOTH, pair_swap)
    gate_kept, up_kept = project(kept)
    pair = jnp.concatenate(
        [
            (gate_kept + got[:, :hidden].astype(jnp.float32)).astype(jnp.bfloat16),
            (up_kept + got[:, hidden:].astype(jnp.float32)).astype(jnp.bfloat16),
        ],
        axis=1,
    )
    parts = exchange(pair.reshape(half // share, share, 2 * hidden), BOTH, team_groups)
    total = jnp.sum(parts.astype(jnp.float32), axis=0)
    active = (jax.nn.silu(total[:, :hidden]) * total[:, hidden:]).astype(jnp.bfloat16)

    copies = jnp.broadcast_to(active[None], (half // share, share, hidden))
    own = exchange(copies, BOTH, team_groups).reshape(half, hidden)
    other = lax.ppermute(own, BOTH, pair_swap)
    own_out = jnp.dot(own, w_down[0], preferred_element_type=jnp.float32).astype(jnp.bfloat16)
    other_out = jnp.dot(other, w_down[0], preferred_element_type=jnp.float32).astype(jnp.bfloat16)
    result = jnp.concatenate(
        [jnp.where(first_team, own_out, other_out), jnp.where(first_team, other_out, own_out)], axis=0
    )
    returned = exchange(result.reshape(chips, CORES * CAP, feat_width), "node", chip_groups)
    swapped = lax.ppermute(returned[:, CAP:].reshape(half, feat_width), "node", core_swap)

    def weigh(weights, rows):
        return lax.dot_general(
            weights,
            rows.astype(jnp.float32),
            (((0,), (0,)), ((), ())),
            precision=lax.Precision.HIGHEST,
        )

    mixed = weigh(combine[:half], returned[:, :CAP].reshape(half, feat_width))
    mixed = mixed + weigh(combine[half:], swapped)
    return mixed.astype(jnp.bfloat16)


def solution(mesh):
    return jax.shard_map(
        body,
        mesh=mesh,
        in_specs=(
            P("node", "local"),
            P("node", None),
            P("node", None),
            P("node", "local", None),
            P("node", "local", None),
            P("node", None, "local"),
        ),
        out_specs=P("node", "local"),
        check_vma=False,
    )
```

```python
import jax
import jax.numpy as jnp
from jax import lax
from jax.sharding import PartitionSpec as P


CAP = 2
CORES = 2
BOTH = ("node", "local")
TEAMS = ((0, 2, 5, 7), (1, 3, 4, 6))
TEAM = (0, 1, 0, 1, 1, 0, 1, 0)


def body(tokens, node_ids, mix_weights, w_gate, w_up, w_down):
    row_count, feat_width = tokens.shape
    node_count = lax.axis_size("node")
    local_count = lax.axis_size("local")
    hidden = w_gate.shape[2]
    members = len(TEAMS[0])
    share = node_count // members

    nodes, places = range(node_count), range(local_count)

    def seat(node, label):
        return node * local_count + (label + node % CORES) % local_count

    def mate(place, core):
        return ((place - core) % local_count ^ 1) + core

    team_groups = [[seat(node, label) for label in team] for node in nodes for team in TEAMS]
    ring_groups = [[seat(node, label) for team in TEAMS for label in team] for node in nodes]
    pair_swap = [(seat(node, label), seat(node, label ^ 1)) for node in nodes for label in places]
    place = lax.axis_index("local")
    slot_of = [
        sum(jnp.where(place == (label + core) % local_count, team, 0) for label, team in enumerate(TEAM))
        for core in range(CORES)
    ]

    def exchange(array, axis, groups=None):
        return lax.all_to_all(
            array, axis, split_axis=0, concat_axis=0, tiled=True, axis_index_groups=groups
        )

    def dot(left, right):
        return jnp.dot(left, right, preferred_element_type=jnp.float32)

    tokens_pair = [
        lax.ppermute(tokens, "local", [(p, mate(p, core) % local_count) for p in places])
        for core in range(CORES)
    ]
    gate_pair = lax.ppermute(w_gate[0], BOTH, pair_swap)
    up_pair = lax.ppermute(w_up[0], BOTH, pair_swap)

    lines = jnp.arange(CAP * node_count, dtype=jnp.int32)[:, None]
    match = node_ids.T[:, None, :] == (lines // CAP)[None]
    hit = jnp.any(match, axis=0)
    weight = jnp.sum(jnp.where(match, mix_weights.T[:, None, :], 0.0), axis=0)
    earlier = jnp.arange(row_count)[:, None] < jnp.arange(row_count)[None, :]
    rank = dot(hit.astype(jnp.bfloat16), earlier.astype(jnp.bfloat16))
    combine = jnp.where(rank == (lines % CAP).astype(jnp.float32), weight, 0.0)
    core_line = lines // CAP % CORES
    slot = jnp.where(core_line == 0, slot_of[0], slot_of[1]).astype(jnp.float32)
    chosen = hit & (rank == slot)
    own_line = lines % CAP == 0
    dispatch = jnp.concatenate(
        [chosen & own_line] + [chosen & ~own_line & (core_line == core) for core in range(CORES)], axis=1
    )

    slices = jnp.concatenate([tokens] + tokens_pair, axis=0)
    outbound = dot(dispatch.astype(jnp.bfloat16), slices).astype(jnp.bfloat16)
    outbound, combine = lax.optimization_barrier((outbound, combine))
    inbound = exchange(outbound.reshape(node_count, CAP, feat_width), "node")
    mine, theirs = inbound[:, 0], inbound[:, 1]
    gate = dot(mine, w_gate[0]) + dot(theirs, gate_pair)
    up = dot(mine, w_up[0]) + dot(theirs, up_pair)
    sums = jnp.concatenate([gate.astype(jnp.bfloat16), up.astype(jnp.bfloat16)], axis=1)
    parts = exchange(sums.reshape(members, share, 2 * hidden), BOTH, team_groups)
    total = jnp.sum(parts.astype(jnp.float32), axis=0)
    active = (jax.nn.silu(total[:, :hidden]) * total[:, hidden:]).astype(jnp.bfloat16)

    copies = jnp.broadcast_to(active[None], (local_count, share, hidden))
    rows = exchange(copies, BOTH, ring_groups).reshape(CAP, node_count, hidden)
    result = jnp.stack([dot(rows[place], w_down[0]).astype(jnp.bfloat16) for place in range(CAP)], axis=1)
    returned = exchange(result, "node").reshape(CAP * node_count, feat_width)
    mixed = lax.dot_general(
        combine,
        returned.astype(jnp.float32),
        (((0,), (0,)), ((), ())),
        precision=lax.Precision.HIGHEST,
    )
    return mixed.astype(jnp.bfloat16)


def solution(mesh):
    return jax.shard_map(
        body,
        mesh=mesh,
        in_specs=(
            P("node", "local"),
            P("node", None),
            P("node", None),
            P("node", "local", None),
            P("node", "local", None),
            P("node", None, "local"),
        ),
        out_specs=P("node", "local"),
        check_vma=False,
    )
```

```python
import jax
import jax.numpy as jnp
from jax import lax
from jax.experimental import pallas as pl
from jax.experimental.pallas import tpu as pltpu
from jax.sharding import PartitionSpec as P


CAP = 2
CORES = 2
BOTH = ("node", "local")
TEAMS = ((0, 2, 5, 7), (1, 3, 4, 6))
TEAM = (0, 1, 0, 1, 1, 0, 1, 0)


def dot(left, right):
    return jnp.dot(left, right, preferred_element_type=jnp.float32)


def one_hot_rows(rows, columns, place, transpose=False):
    line = lax.broadcasted_iota(jnp.int32, (rows, columns), 0)
    column = lax.broadcasted_iota(jnp.int32, (rows, columns), 1)
    same = line == column * CAP + place if transpose else column == line * CAP + place
    return same.astype(jnp.float32).astype(jnp.bfloat16)


def route_kernel(slot_ref, ids_ref, mix_ref, own_ref, first_ref, second_ref, out_ref, high_ref, low_ref):
    lines, row_count = high_ref.shape
    line = lax.broadcasted_iota(jnp.int32, (lines, row_count), 0)
    expert, part = line // CAP, line % CAP
    parity = expert % CORES
    hit = jnp.zeros((lines, row_count), jnp.float32)
    weight = jnp.zeros((lines, row_count), jnp.float32)
    for pick in range(ids_ref.shape[0]):
        match = ids_ref[pick : pick + 1, :] == expert
        hit = jnp.where(match, 1.0, hit)
        weight = jnp.where(match, mix_ref[pick : pick + 1, :], weight)
    before = lax.broadcasted_iota(jnp.int32, (row_count, row_count), 0)
    after = lax.broadcasted_iota(jnp.int32, (row_count, row_count), 1)
    earlier = jnp.where(before < after, 1.0, 0.0).astype(jnp.bfloat16)
    rank = dot(hit.astype(jnp.bfloat16), earlier)
    combine = jnp.where(rank == part.astype(jnp.float32), weight, 0.0)
    high = combine.astype(jnp.bfloat16)
    high_ref[...] = high
    low_ref[...] = (combine - high.astype(jnp.float32)).astype(jnp.bfloat16)
    slot = jnp.where(parity == 0, slot_ref[0], slot_ref[1]).astype(jnp.float32)
    chosen = jnp.where(rank == slot, hit, 0.0)
    total = dot(jnp.where(part == 0, chosen, 0.0).astype(jnp.bfloat16), own_ref[...])
    theirs = jnp.where(part == 1, chosen, 0.0)
    for core, ref in enumerate((first_ref, second_ref)):
        total = total + dot(jnp.where(parity == core, theirs, 0.0).astype(jnp.bfloat16), ref[...])
    out_ref[...] = total.astype(jnp.bfloat16)


def project_kernel(rows_ref, own_ref, pair_ref, out_ref):
    lines = rows_ref.shape[0]
    rows = rows_ref[...]
    mine = dot(one_hot_rows(lines // CAP, lines, 0), rows).astype(jnp.bfloat16)
    theirs = dot(one_hot_rows(lines // CAP, lines, 1), rows).astype(jnp.bfloat16)
    out_ref[...] = (dot(mine, own_ref[...]) + dot(theirs, pair_ref[...])).astype(jnp.bfloat16)


def down_kernel(rows_ref, w_ref, out_ref):
    half = rows_ref.shape[0] // CAP
    total = 0.0
    for place in range(CAP):
        result = dot(rows_ref[place * half : (place + 1) * half, :], w_ref[...]).astype(jnp.bfloat16)
        total = total + dot(one_hot_rows(CAP * half, half, place, True), result)
    out_ref[...] = total.astype(jnp.bfloat16)


def combine_kernel(high_ref, low_ref, rows_ref, out_ref):
    rows = rows_ref[...]
    total = 0.0
    for ref in (high_ref, low_ref):
        total = total + lax.dot_general(
            ref[...], rows, (((0,), (0,)), ((), ())), preferred_element_type=jnp.float32
        )
    out_ref[...] = total.astype(jnp.bfloat16)


def run(kernel, shapes, *operands, final=False):
    specs = [
        pl.BlockSpec(memory_space=pltpu.SMEM if array.ndim == 1 else pltpu.VMEM) for array in operands
    ]
    operands = [
        array if array.ndim == 1 else pltpu.with_memory_space_constraint(array, pltpu.VMEM)
        for array in operands
    ]
    outs = [
        jax.ShapeDtypeStruct(shape, jnp.bfloat16) if final else pltpu.VMEM(shape, jnp.bfloat16)
        for shape in shapes
    ]
    result = pl.pallas_call(
        kernel,
        in_specs=specs,
        out_specs=[pl.BlockSpec(memory_space=pltpu.VMEM)] * len(outs),
        out_shape=outs,
        compiler_params=pltpu.CompilerParams(vmem_limit_bytes=16 << 20),
    )(*operands)
    return result if len(outs) > 1 else result[0]


def body(tokens, node_ids, mix_weights, w_gate, w_up, w_down):
    row_count, feat_width = tokens.shape
    node_count = lax.axis_size("node")
    local_count = lax.axis_size("local")
    hidden = w_gate.shape[2]
    members = len(TEAMS[0])
    share = node_count // members

    nodes, places = range(node_count), range(local_count)

    def seat(node, label):
        return node * local_count + (label + node % CORES) % local_count

    def mate(place, core):
        return ((place - core) % local_count ^ 1) + core

    team_groups = [[seat(node, label) for label in team] for node in nodes for team in TEAMS]
    ring_groups = [[seat(node, label) for team in TEAMS for label in team] for node in nodes]
    pair_swap = [(seat(node, label), seat(node, label ^ 1)) for node in nodes for label in places]
    place = lax.axis_index("local")
    slot_of = [
        sum(jnp.where(place == (label + core) % local_count, team, 0) for label, team in enumerate(TEAM))
        for core in range(CORES)
    ]

    def exchange(array, axis, groups=None):
        return lax.all_to_all(
            array, axis, split_axis=0, concat_axis=0, tiled=True, axis_index_groups=groups
        )

    tokens_pair = [
        lax.ppermute(tokens, "local", [(p, mate(p, core) % local_count) for p in places])
        for core in range(CORES)
    ]
    w_own = jnp.concatenate([w_gate[0], w_up[0]], axis=1)
    w_pair = lax.ppermute(w_own, BOTH, pair_swap)

    lines = CAP * node_count
    outbound, high, low = run(
        route_kernel,
        [(lines, feat_width), (lines, row_count), (lines, row_count)],
        jnp.stack(slot_of).astype(jnp.int32),
        node_ids.T,
        mix_weights.T,
        tokens,
        *tokens_pair,
    )
    inbound = exchange(outbound.reshape(node_count, CAP, feat_width), "node")
    sums = run(
        project_kernel, [(node_count, 2 * hidden)], inbound.reshape(lines, feat_width), w_own, w_pair
    )
    parts = exchange(sums.reshape(members, share, 2 * hidden), BOTH, team_groups)
    total = jnp.sum(parts.astype(jnp.float32), axis=0)
    active = (jax.nn.silu(total[:, :hidden]) * total[:, hidden:]).astype(jnp.bfloat16)

    copies = jnp.broadcast_to(active[None], (local_count, share, hidden))
    rows = exchange(copies, BOTH, ring_groups).reshape(lines, hidden)
    result = run(down_kernel, [(lines, feat_width)], rows, w_down[0])
    returned = exchange(result.reshape(node_count, CAP, feat_width), "node").reshape(lines, feat_width)
    return run(combine_kernel, [(row_count, feat_width)], high, low, returned, final=True)


def solution(mesh):
    return jax.shard_map(
        body,
        mesh=mesh,
        in_specs=(
            P("node", "local"),
            P("node", None),
            P("node", None),
            P("node", "local", None),
            P("node", "local", None),
            P("node", None, "local"),
        ),
        out_specs=P("node", "local"),
        check_vma=False,
    )
```

```python
import jax
import jax.numpy as jnp
from jax import lax
from jax.experimental import pallas as pl
from jax.experimental.pallas import tpu as pltpu
from jax.sharding import PartitionSpec as P


CAP = 2
CORES = 2
BOTH = ("node", "local")
TEAMS = ((0, 2, 5, 7), (1, 3, 4, 6))
TEAM = (0, 1, 0, 1, 1, 0, 1, 0)


def dot(left, right):
    return jnp.dot(left, right, preferred_element_type=jnp.float32)


def one_hot_rows(rows, columns, place, transpose=False):
    line = lax.broadcasted_iota(jnp.int32, (rows, columns), 0)
    column = lax.broadcasted_iota(jnp.int32, (rows, columns), 1)
    same = line == column * CAP + place if transpose else column == line * CAP + place
    return same.astype(jnp.float32).astype(jnp.bfloat16)


def prepare_kernel(
    meta_ref, ids_hbm, mix_hbm, gate_ref, up_ref,
    joined_ref, own_ref, first_ref, second_ref, high_ref, low_ref,
    ids_ref, mix_ref, sems,
):
    hidden = gate_ref.shape[1]
    tables = [
        pltpu.make_async_copy(source, target, sems.at[2 + index])
        for index, (source, target) in enumerate(((ids_hbm, ids_ref), (mix_hbm, mix_ref)))
    ]
    for table in tables:
        table.start()
    joins = [
        pltpu.make_async_copy(ref, joined_ref.at[:, pl.ds(index * hidden, hidden)], sems.at[index])
        for index, ref in enumerate((gate_ref, up_ref))
    ]
    for join in joins:
        join.start()
    for table in tables:
        table.wait()
    lines, row_count = high_ref.shape
    line = lax.broadcasted_iota(jnp.int32, (lines, row_count), 0)
    expert, part = line // CAP, line % CAP
    parity = expert % CORES
    hit = jnp.zeros((lines, row_count), jnp.float32)
    weight = jnp.zeros((lines, row_count), jnp.float32)
    for pick in range(ids_ref.shape[0]):
        match = ids_ref[pick : pick + 1, :] == expert
        hit = jnp.where(match, 1.0, hit)
        weight = jnp.where(match, mix_ref[pick : pick + 1, :], weight)
    before = lax.broadcasted_iota(jnp.int32, (row_count, row_count), 0)
    after = lax.broadcasted_iota(jnp.int32, (row_count, row_count), 1)
    earlier = jnp.where(before < after, 1.0, 0.0).astype(jnp.bfloat16)
    rank = dot(hit.astype(jnp.bfloat16), earlier)
    combine = jnp.where(rank == part.astype(jnp.float32), weight, 0.0)
    high = combine.astype(jnp.bfloat16)
    high_ref[...] = high
    low_ref[...] = (combine - high.astype(jnp.float32)).astype(jnp.bfloat16)
    slot = jnp.where(parity == 0, meta_ref[0], meta_ref[1]).astype(jnp.float32)
    chosen = jnp.where(rank == slot, hit, 0.0)
    own_ref[...] = jnp.where(part == 0, chosen, 0.0).astype(jnp.bfloat16)
    theirs = jnp.where(part == 1, chosen, 0.0)
    for core, ref in enumerate((first_ref, second_ref)):
        ref[...] = jnp.where(parity == core, theirs, 0.0).astype(jnp.bfloat16)
    for join in joins:
        join.wait()


def gather_kernel(*refs):
    out_ref = refs[-1]
    picks, slices = refs[: len(refs) // 2], refs[len(refs) // 2 : -1]
    total = sum(dot(pick[...], rows[...]) for pick, rows in zip(picks, slices))
    out_ref[...] = total.astype(jnp.bfloat16)


def project_kernel(rows_ref, own_ref, pair_ref, out_ref, total_ref, pair_buf, sem):
    copy = pltpu.make_async_copy(pair_ref, pair_buf, sem)
    copy.start()
    lines = rows_ref.shape[0]
    rows = rows_ref[...]
    mine = dot(one_hot_rows(lines // CAP, lines, 0), rows).astype(jnp.bfloat16)
    theirs = dot(one_hot_rows(lines // CAP, lines, 1), rows).astype(jnp.bfloat16)
    total_ref[...] = dot(mine, own_ref[...])
    copy.wait()
    out_ref[...] = (total_ref[...] + dot(theirs, pair_buf[...])).astype(jnp.bfloat16)


def down_kernel(meta_ref, rows_ref, w_ref, out_ref, result_ref):
    lines = rows_ref.shape[0]
    ring = len(TEAM)
    share = lines // ring
    core = meta_ref[2]
    result_ref[...] = dot(rows_ref[...], w_ref[...]).astype(jnp.bfloat16)
    for member in range(len(TEAMS[0])):
        total = 0.0
        for place, team in enumerate(TEAMS):
            seat = lax.rem(team[member] + core, ring)
            block = result_ref[pl.ds(pl.multiple_of(seat * share, share), share), :]
            total = total + dot(one_hot_rows(CAP * share, share, place, True), block)
        out_ref[member * CAP * share : (member + 1) * CAP * share, :] = total.astype(jnp.bfloat16)


def combine_kernel(high_ref, low_ref, rows_ref, out_ref):
    rows = rows_ref[...]
    total = 0.0
    for ref in (high_ref, low_ref):
        total = total + lax.dot_general(
            ref[...], rows, (((0,), (0,)), ((), ())), preferred_element_type=jnp.float32
        )
    out_ref[...] = total.astype(jnp.bfloat16)


def run(kernel, shapes, *operands, hbm=(), scratch=(), final=False):
    specs, placed = [], []
    for index, array in enumerate(operands):
        if array.ndim == 1:
            specs.append(pl.BlockSpec(memory_space=pltpu.SMEM))
        elif index in hbm:
            specs.append(pl.BlockSpec(memory_space=pltpu.HBM))
            array = pltpu.with_memory_space_constraint(array, pltpu.HBM)
        else:
            specs.append(pl.BlockSpec(memory_space=pltpu.VMEM))
            array = pltpu.with_memory_space_constraint(array, pltpu.VMEM)
        placed.append(array)
    outs = [
        jax.ShapeDtypeStruct(shape, jnp.bfloat16) if final else pltpu.VMEM(shape, jnp.bfloat16)
        for shape in shapes
    ]
    result = pl.pallas_call(
        kernel,
        in_specs=specs,
        out_specs=[pl.BlockSpec(memory_space=pltpu.VMEM)] * len(outs),
        out_shape=outs,
        scratch_shapes=list(scratch),
        compiler_params=pltpu.CompilerParams(vmem_limit_bytes=16 << 20),
    )(*placed)
    return result if len(outs) > 1 else result[0]


def body(tokens, node_ids, mix_weights, w_gate, w_up, w_down):
    row_count, feat_width = tokens.shape
    node_count = lax.axis_size("node")
    local_count = lax.axis_size("local")
    hidden = w_gate.shape[2]
    members = len(TEAMS[0])
    share = node_count // members

    nodes, places = range(node_count), range(local_count)

    def seat(node, label):
        return node * local_count + (label + node % CORES) % local_count

    def mate(place, core):
        return ((place - core) % local_count ^ 1) + core

    team_groups = [[seat(node, label) for label in team] for node in nodes for team in TEAMS]
    pair_swap = [(seat(node, label), seat(node, label ^ 1)) for node in nodes for label in places]
    place = lax.axis_index("local")
    slot_of = [
        sum(jnp.where(place == (label + core) % local_count, team, 0) for label, team in enumerate(TEAM))
        for core in range(CORES)
    ]

    def exchange(array, axis, groups=None):
        return lax.all_to_all(
            array, axis, split_axis=0, concat_axis=0, tiled=True, axis_index_groups=groups
        )

    tokens_pair = [
        lax.ppermute(tokens, "local", [(p, mate(p, core) % local_count) for p in places])
        for core in range(CORES)
    ]
    lines = CAP * node_count
    core = lax.axis_index("node") % CORES
    meta = jnp.stack(slot_of + [core]).astype(jnp.int32)
    w_own, *tables = run(
        prepare_kernel,
        [(feat_width, 2 * hidden)] + [(lines, row_count)] * 5,
        meta,
        node_ids.T,
        mix_weights.T,
        w_gate[0],
        w_up[0],
        hbm=(1, 2, 3, 4),
        scratch=[
            pltpu.VMEM(node_ids.shape[::-1], jnp.int32),
            pltpu.VMEM(mix_weights.shape[::-1], jnp.float32),
            pltpu.SemaphoreType.DMA((4,)),
        ],
    )
    picks, (high, low) = tables[:3], tables[3:]
    w_pair = lax.ppermute(w_own, BOTH, pair_swap)
    outbound = run(gather_kernel, [(lines, feat_width)], *picks, tokens, *tokens_pair)
    inbound = exchange(outbound.reshape(node_count, CAP, feat_width), "node")
    sums = run(
        project_kernel,
        [(node_count, 2 * hidden)],
        inbound.reshape(lines, feat_width),
        w_own,
        w_pair,
        hbm=(2,),
        scratch=[
            pltpu.VMEM((node_count, 2 * hidden), jnp.float32),
            pltpu.VMEM((feat_width, 2 * hidden), jnp.bfloat16),
            pltpu.SemaphoreType.DMA,
        ],
    )
    parts = exchange(sums.reshape(members, share, 2 * hidden), BOTH, team_groups)
    total = jnp.sum(parts.astype(jnp.float32), axis=0)
    active = (jax.nn.silu(total[:, :hidden]) * total[:, hidden:]).astype(jnp.bfloat16)

    copies = jnp.broadcast_to(active[None], (local_count, share, hidden))
    rows = exchange(copies, "local").reshape(lines, hidden)
    result = run(
        down_kernel,
        [(lines, feat_width)],
        meta,
        rows,
        w_down[0],
        scratch=[pltpu.VMEM((lines, feat_width), jnp.bfloat16)],
    )
    returned = exchange(result.reshape(node_count, CAP, feat_width), "node").reshape(lines, feat_width)
    return run(combine_kernel, [(row_count, feat_width)], high, low, returned, final=True)


def solution(mesh):
    return jax.shard_map(
        body,
        mesh=mesh,
        in_specs=(
            P("node", "local"),
            P("node", None),
            P("node", None),
            P("node", "local", None),
            P("node", "local", None),
            P("node", None, "local"),
        ),
        out_specs=P("node", "local"),
        check_vma=False,
    )
```

```python
import jax
import jax.numpy as jnp
from jax import lax
from jax.experimental import pallas as pl
from jax.experimental.pallas import tpu as pltpu
from jax.sharding import PartitionSpec as P


CAP = 2
CORES = 2
BOTH = ("node", "local")
TEAMS = ((0, 2, 5, 7), (1, 3, 4, 6))
TEAM = (0, 1, 0, 1, 1, 0, 1, 0)


def dot(left, right):
    return jnp.dot(left, right, preferred_element_type=jnp.float32)


def one_hot_rows(rows, columns, place, transpose=False):
    line = lax.broadcasted_iota(jnp.int32, (rows, columns), 0)
    column = lax.broadcasted_iota(jnp.int32, (rows, columns), 1)
    same = line == column * CAP + place if transpose else column == line * CAP + place
    return same.astype(jnp.float32).astype(jnp.bfloat16)


def prepare_kernel(
    meta_ref, ids_hbm, mix_hbm, gate_ref, up_ref,
    joined_ref, own_ref, first_ref, second_ref, high_ref, low_ref,
    ids_ref, mix_ref, sems,
):
    hidden = gate_ref.shape[1]
    tables = [
        pltpu.make_async_copy(source, target, sems.at[2 + index])
        for index, (source, target) in enumerate(((ids_hbm, ids_ref), (mix_hbm, mix_ref)))
    ]
    for table in tables:
        table.start()
    joins = [
        pltpu.make_async_copy(ref, joined_ref.at[:, pl.ds(index * hidden, hidden)], sems.at[index])
        for index, ref in enumerate((gate_ref, up_ref))
    ]
    for join in joins:
        join.start()
    for table in tables:
        table.wait()
    lines, row_count = high_ref.shape
    line = lax.broadcasted_iota(jnp.int32, (lines, row_count), 0)
    expert, part = line // CAP, line % CAP
    parity = expert % CORES
    hit = jnp.zeros((lines, row_count), jnp.float32)
    weight = jnp.zeros((lines, row_count), jnp.float32)
    for pick in range(ids_ref.shape[0]):
        match = ids_ref[pick : pick + 1, :] == expert
        hit = jnp.where(match, 1.0, hit)
        weight = jnp.where(match, mix_ref[pick : pick + 1, :], weight)
    before = lax.broadcasted_iota(jnp.int32, (row_count, row_count), 0)
    after = lax.broadcasted_iota(jnp.int32, (row_count, row_count), 1)
    earlier = jnp.where(before < after, 1.0, 0.0).astype(jnp.bfloat16)
    rank = dot(hit.astype(jnp.bfloat16), earlier)
    combine = jnp.where(rank == part.astype(jnp.float32), weight, 0.0)
    high = combine.astype(jnp.bfloat16)
    high_ref[...] = high
    low_ref[...] = (combine - high.astype(jnp.float32)).astype(jnp.bfloat16)
    slot = jnp.where(parity == 0, meta_ref[0], meta_ref[1]).astype(jnp.float32)
    chosen = jnp.where(rank == slot, hit, 0.0)
    own_ref[...] = jnp.where(part == 0, chosen, 0.0).astype(jnp.bfloat16)
    theirs = jnp.where(part == 1, chosen, 0.0)
    for core, ref in enumerate((first_ref, second_ref)):
        ref[...] = jnp.where(parity == core, theirs, 0.0).astype(jnp.bfloat16)
    for join in joins:
        join.wait()


def gather_kernel(*refs):
    out_ref = refs[-1]
    picks, slices = refs[: len(refs) // 2], refs[len(refs) // 2 : -1]
    total = sum(dot(pick[...], rows[...]) for pick, rows in zip(picks, slices))
    out_ref[...] = total.astype(jnp.bfloat16)


def project_kernel(rows_ref, own_ref, pair_ref, out_ref, total_ref, pair_buf, sem):
    copy = pltpu.make_async_copy(pair_ref, pair_buf, sem)
    copy.start()
    lines = rows_ref.shape[0]
    rows = rows_ref[...]
    mine = dot(one_hot_rows(lines // CAP, lines, 0), rows).astype(jnp.bfloat16)
    theirs = dot(one_hot_rows(lines // CAP, lines, 1), rows).astype(jnp.bfloat16)
    total_ref[...] = dot(mine, own_ref[...])
    copy.wait()
    out_ref[...] = (total_ref[...] + dot(theirs, pair_buf[...])).astype(jnp.bfloat16)


def down_kernel(rows_ref, w_ref, out_ref):
    half = rows_ref.shape[0] // CAP
    total = 0.0
    for place in range(CAP):
        result = dot(rows_ref[place * half : (place + 1) * half, :], w_ref[...]).astype(jnp.bfloat16)
        total = total + dot(one_hot_rows(CAP * half, half, place, True), result)
    out_ref[...] = total.astype(jnp.bfloat16)


def combine_kernel(high_ref, low_ref, rows_ref, out_ref):
    rows = rows_ref[...]
    total = 0.0
    for ref in (high_ref, low_ref):
        total = total + lax.dot_general(
            ref[...], rows, (((0,), (0,)), ((), ())), preferred_element_type=jnp.float32
        )
    out_ref[...] = total.astype(jnp.bfloat16)


def run(kernel, shapes, *operands, hbm=(), scratch=(), final=False):
    specs, placed = [], []
    for index, array in enumerate(operands):
        if array.ndim == 1:
            specs.append(pl.BlockSpec(memory_space=pltpu.SMEM))
        elif index in hbm:
            specs.append(pl.BlockSpec(memory_space=pltpu.HBM))
            array = pltpu.with_memory_space_constraint(array, pltpu.HBM)
        else:
            specs.append(pl.BlockSpec(memory_space=pltpu.VMEM))
            array = pltpu.with_memory_space_constraint(array, pltpu.VMEM)
        placed.append(array)
    outs = [
        jax.ShapeDtypeStruct(shape, jnp.bfloat16) if final else pltpu.VMEM(shape, jnp.bfloat16)
        for shape in shapes
    ]
    result = pl.pallas_call(
        kernel,
        in_specs=specs,
        out_specs=[pl.BlockSpec(memory_space=pltpu.VMEM)] * len(outs),
        out_shape=outs,
        scratch_shapes=list(scratch),
        compiler_params=pltpu.CompilerParams(vmem_limit_bytes=16 << 20),
    )(*placed)
    return result if len(outs) > 1 else result[0]


def body(tokens, node_ids, mix_weights, w_gate, w_up, w_down):
    row_count, feat_width = tokens.shape
    node_count = lax.axis_size("node")
    local_count = lax.axis_size("local")
    hidden = w_gate.shape[2]
    members = len(TEAMS[0])
    share = node_count // members

    nodes, places = range(node_count), range(local_count)

    def seat(node, label):
        return node * local_count + (label + node % CORES) % local_count

    def mate(place, core):
        return ((place - core) % local_count ^ 1) + core

    team_groups = [[seat(node, label) for label in team] for node in nodes for team in TEAMS]
    ring_groups = [[seat(node, label) for team in TEAMS for label in team] for node in nodes]
    pair_swap = [(seat(node, label), seat(node, label ^ 1)) for node in nodes for label in places]
    place = lax.axis_index("local")
    slot_of = [
        sum(jnp.where(place == (label + core) % local_count, team, 0) for label, team in enumerate(TEAM))
        for core in range(CORES)
    ]

    def exchange(array, axis, groups=None):
        return lax.all_to_all(
            array, axis, split_axis=0, concat_axis=0, tiled=True, axis_index_groups=groups
        )

    tokens_pair = [
        lax.ppermute(tokens, "local", [(p, mate(p, core) % local_count) for p in places])
        for core in range(CORES)
    ]
    lines = CAP * node_count
    meta = jnp.stack(slot_of).astype(jnp.int32)
    w_own, *tables = run(
        prepare_kernel,
        [(feat_width, 2 * hidden)] + [(lines, row_count)] * 5,
        meta,
        node_ids.T,
        mix_weights.T,
        w_gate[0],
        w_up[0],
        hbm=(1, 2, 3, 4),
        scratch=[
            pltpu.VMEM(node_ids.shape[::-1], jnp.int32),
            pltpu.VMEM(mix_weights.shape[::-1], jnp.float32),
            pltpu.SemaphoreType.DMA((4,)),
        ],
    )
    picks, (high, low) = tables[:3], tables[3:]
    w_pair = lax.ppermute(w_own, BOTH, pair_swap)
    outbound = run(gather_kernel, [(lines, feat_width)], *picks, tokens, *tokens_pair)
    inbound = exchange(outbound.reshape(node_count, CAP, feat_width), "node")
    sums = run(
        project_kernel,
        [(node_count, 2 * hidden)],
        inbound.reshape(lines, feat_width),
        w_own,
        w_pair,
        hbm=(2,),
        scratch=[
            pltpu.VMEM((node_count, 2 * hidden), jnp.float32),
            pltpu.VMEM((feat_width, 2 * hidden), jnp.bfloat16),
            pltpu.SemaphoreType.DMA,
        ],
    )
    parts = exchange(sums.reshape(members, share, 2 * hidden), BOTH, team_groups)
    total = jnp.sum(parts.astype(jnp.float32), axis=0)
    active = (jax.nn.silu(total[:, :hidden]) * total[:, hidden:]).astype(jnp.bfloat16)

    copies = jnp.broadcast_to(active[None], (local_count, share, hidden))
    rows = exchange(copies, BOTH, ring_groups).reshape(lines, hidden)
    result = run(down_kernel, [(lines, feat_width)], rows, w_down[0])
    returned = exchange(result.reshape(node_count, CAP, feat_width), "node").reshape(lines, feat_width)
    return run(combine_kernel, [(row_count, feat_width)], high, low, returned, final=True)


def solution(mesh):
    return jax.shard_map(
        body,
        mesh=mesh,
        in_specs=(
            P("node", "local"),
            P("node", None),
            P("node", None),
            P("node", "local", None),
            P("node", "local", None),
            P("node", None, "local"),
        ),
        out_specs=P("node", "local"),
        check_vma=False,
    )
```

```python
import jax
import jax.numpy as jnp
from jax import lax
from jax.experimental import pallas as pl
from jax.experimental.pallas import tpu as pltpu
from jax.sharding import PartitionSpec as P


CAP = 2
CORES = 2
BOTH = ("node", "local")
TEAMS = ((0, 2, 5, 7), (1, 3, 4, 6))
TEAM = (0, 1, 0, 1, 1, 0, 1, 0)


def dot(left, right):
    return jnp.dot(left, right, preferred_element_type=jnp.float32)


def one_hot_rows(rows, columns, place, transpose=False):
    line = lax.broadcasted_iota(jnp.int32, (rows, columns), 0)
    column = lax.broadcasted_iota(jnp.int32, (rows, columns), 1)
    same = line == column * CAP + place if transpose else column == line * CAP + place
    return same.astype(jnp.float32).astype(jnp.bfloat16)


def tables_kernel(
    meta_ref, ids_hbm, mix_hbm, own_ref, first_ref, second_ref, high_ref, low_ref, ids_ref, mix_ref, sems
):
    tables = [
        pltpu.make_async_copy(source, target, sems.at[index])
        for index, (source, target) in enumerate(((ids_hbm, ids_ref), (mix_hbm, mix_ref)))
    ]
    for table in tables:
        table.start()
    for table in tables:
        table.wait()
    lines, row_count = high_ref.shape
    line = lax.broadcasted_iota(jnp.int32, (lines, row_count), 0)
    expert, part = line // CAP, line % CAP
    parity = expert % CORES
    hit = jnp.zeros((lines, row_count), jnp.float32)
    weight = jnp.zeros((lines, row_count), jnp.float32)
    for pick in range(ids_ref.shape[0]):
        match = ids_ref[pick : pick + 1, :] == expert
        hit = jnp.where(match, 1.0, hit)
        weight = jnp.where(match, mix_ref[pick : pick + 1, :], weight)
    before = lax.broadcasted_iota(jnp.int32, (row_count, row_count), 0)
    after = lax.broadcasted_iota(jnp.int32, (row_count, row_count), 1)
    earlier = jnp.where(before < after, 1.0, 0.0).astype(jnp.bfloat16)
    rank = dot(hit.astype(jnp.bfloat16), earlier)
    combine = jnp.where(rank == part.astype(jnp.float32), weight, 0.0)
    high = combine.astype(jnp.bfloat16)
    high_ref[...] = high
    low_ref[...] = (combine - high.astype(jnp.float32)).astype(jnp.bfloat16)
    slot = jnp.where(parity == 0, meta_ref[0], meta_ref[1]).astype(jnp.float32)
    chosen = jnp.where(rank == slot, hit, 0.0)
    own_ref[...] = jnp.where(part == 0, chosen, 0.0).astype(jnp.bfloat16)
    theirs = jnp.where(part == 1, chosen, 0.0)
    for core, ref in enumerate((first_ref, second_ref)):
        ref[...] = jnp.where(parity == core, theirs, 0.0).astype(jnp.bfloat16)


def gather_kernel(*refs):
    out_ref = refs[-1]
    picks, slices = refs[: len(refs) // 2], refs[len(refs) // 2 : -1]
    total = sum(dot(pick[...], rows[...]) for pick, rows in zip(picks, slices))
    out_ref[...] = total.astype(jnp.bfloat16)


def project_kernel(rows_ref, *refs):
    own, pair, (out_ref, total_ref), bufs, sems = refs[:2], refs[2:4], refs[4:6], refs[6:8], refs[8]
    copies = [
        pltpu.make_async_copy(source, target, sems.at[index])
        for index, (source, target) in enumerate(zip(pair, bufs))
    ]
    for copy in copies:
        copy.start()
    lines = rows_ref.shape[0]
    hidden = bufs[0].shape[1]
    rows = rows_ref[...]
    mine = dot(one_hot_rows(lines // CAP, lines, 0), rows).astype(jnp.bfloat16)
    theirs = dot(one_hot_rows(lines // CAP, lines, 1), rows).astype(jnp.bfloat16)
    for index, ref in enumerate(own):
        total_ref[:, index * hidden : (index + 1) * hidden] = dot(mine, ref[...])
    for index, (copy, buf) in enumerate(zip(copies, bufs)):
        columns = slice(index * hidden, (index + 1) * hidden)
        copy.wait()
        out_ref[:, columns] = (total_ref[:, columns] + dot(theirs, buf[...])).astype(jnp.bfloat16)


def down_kernel(rows_ref, w_ref, out_ref):
    half = rows_ref.shape[0] // CAP
    total = 0.0
    for place in range(CAP):
        result = dot(rows_ref[place * half : (place + 1) * half, :], w_ref[...]).astype(jnp.bfloat16)
        total = total + dot(one_hot_rows(CAP * half, half, place, True), result)
    out_ref[...] = total.astype(jnp.bfloat16)


def combine_kernel(high_ref, low_ref, rows_ref, out_ref):
    rows = rows_ref[...]
    total = 0.0
    for ref in (high_ref, low_ref):
        total = total + lax.dot_general(
            ref[...], rows, (((0,), (0,)), ((), ())), preferred_element_type=jnp.float32
        )
    out_ref[...] = total.astype(jnp.bfloat16)


def run(kernel, shapes, *operands, hbm=(), scratch=(), final=False):
    specs, placed = [], []
    for index, array in enumerate(operands):
        if array.ndim == 1:
            specs.append(pl.BlockSpec(memory_space=pltpu.SMEM))
        elif index in hbm:
            specs.append(pl.BlockSpec(memory_space=pltpu.HBM))
            array = pltpu.with_memory_space_constraint(array, pltpu.HBM)
        else:
            specs.append(pl.BlockSpec(memory_space=pltpu.VMEM))
            array = pltpu.with_memory_space_constraint(array, pltpu.VMEM)
        placed.append(array)
    outs = [
        jax.ShapeDtypeStruct(shape, jnp.bfloat16) if final else pltpu.VMEM(shape, jnp.bfloat16)
        for shape in shapes
    ]
    result = pl.pallas_call(
        kernel,
        in_specs=specs,
        out_specs=[pl.BlockSpec(memory_space=pltpu.VMEM)] * len(outs),
        out_shape=outs,
        scratch_shapes=list(scratch),
        compiler_params=pltpu.CompilerParams(vmem_limit_bytes=16 << 20),
    )(*placed)
    return result if len(outs) > 1 else result[0]


def body(tokens, node_ids, mix_weights, w_gate, w_up, w_down):
    row_count, feat_width = tokens.shape
    node_count = lax.axis_size("node")
    local_count = lax.axis_size("local")
    hidden = w_gate.shape[2]
    members = len(TEAMS[0])
    share = node_count // members

    nodes, places = range(node_count), range(local_count)

    def seat(node, label):
        return node * local_count + (label + node % CORES) % local_count

    def mate(place, core):
        return ((place - core) % local_count ^ 1) + core

    team_groups = [[seat(node, label) for label in team] for node in nodes for team in TEAMS]
    ring_groups = [[seat(node, label) for team in TEAMS for label in team] for node in nodes]
    pair_swap = [(seat(node, label), seat(node, label ^ 1)) for node in nodes for label in places]
    place = lax.axis_index("local")
    slot_of = [
        sum(jnp.where(place == (label + core) % local_count, team, 0) for label, team in enumerate(TEAM))
        for core in range(CORES)
    ]

    def exchange(array, axis, groups=None):
        return lax.all_to_all(
            array, axis, split_axis=0, concat_axis=0, tiled=True, axis_index_groups=groups
        )

    gate_pair = lax.ppermute(w_gate[0], BOTH, pair_swap)
    up_pair = lax.ppermute(w_up[0], BOTH, pair_swap)
    tokens_pair = [
        lax.ppermute(tokens, "local", [(p, mate(p, core) % local_count) for p in places])
        for core in range(CORES)
    ]
    lines = CAP * node_count
    meta = jnp.stack(slot_of).astype(jnp.int32)
    *picks, high, low = run(
        tables_kernel,
        [(lines, row_count)] * 5,
        meta,
        node_ids.T,
        mix_weights.T,
        hbm=(1, 2),
        scratch=[
            pltpu.VMEM(node_ids.shape[::-1], jnp.int32),
            pltpu.VMEM(mix_weights.shape[::-1], jnp.float32),
            pltpu.SemaphoreType.DMA((2,)),
        ],
    )
    outbound = run(gather_kernel, [(lines, feat_width)], *picks, tokens, *tokens_pair)
    inbound = exchange(outbound.reshape(node_count, CAP, feat_width), "node")
    sums = run(
        project_kernel,
        [(node_count, 2 * hidden)],
        inbound.reshape(lines, feat_width),
        w_gate[0],
        w_up[0],
        gate_pair,
        up_pair,
        hbm=(3, 4),
        scratch=[
            pltpu.VMEM((node_count, 2 * hidden), jnp.float32),
            pltpu.VMEM((feat_width, hidden), jnp.bfloat16),
            pltpu.VMEM((feat_width, hidden), jnp.bfloat16),
            pltpu.SemaphoreType.DMA((2,)),
        ],
    )
    parts = exchange(sums.reshape(members, share, 2 * hidden), BOTH, team_groups)
    total = jnp.sum(parts.astype(jnp.float32), axis=0)
    active = (jax.nn.silu(total[:, :hidden]) * total[:, hidden:]).astype(jnp.bfloat16)

    copies = jnp.broadcast_to(active[None], (local_count, share, hidden))
    rows = exchange(copies, BOTH, ring_groups).reshape(lines, hidden)
    result = run(down_kernel, [(lines, feat_width)], rows, w_down[0])
    returned = exchange(result.reshape(node_count, CAP, feat_width), "node").reshape(lines, feat_width)
    return run(combine_kernel, [(row_count, feat_width)], high, low, returned, final=True)


def solution(mesh):
    return jax.shard_map(
        body,
        mesh=mesh,
        in_specs=(
            P("node", "local"),
            P("node", None),
            P("node", None),
            P("node", "local", None),
            P("node", "local", None),
            P("node", None, "local"),
        ),
        out_specs=P("node", "local"),
        check_vma=False,
    )
```

```python
import jax
import jax.numpy as jnp
from jax import lax
from jax.experimental import pallas as pl
from jax.experimental.pallas import tpu as pltpu
from jax.sharding import PartitionSpec as P


CAP = 2
CORES = 2
BOTH = ("node", "local")
TEAMS = ((0, 2, 5, 7), (1, 3, 4, 6))
TEAM = (0, 1, 0, 1, 1, 0, 1, 0)


def dot(left, right):
    return jnp.dot(left, right, preferred_element_type=jnp.float32)


def one_hot_rows(rows, columns, place, transpose=False):
    line = lax.broadcasted_iota(jnp.int32, (rows, columns), 0)
    column = lax.broadcasted_iota(jnp.int32, (rows, columns), 1)
    same = line == column * CAP + place if transpose else column == line * CAP + place
    return same.astype(jnp.float32).astype(jnp.bfloat16)


def route_kernel(
    slot_ref, ids_hbm, mix_hbm, own_ref, first_ref, second_ref, out_ref, high_ref, low_ref, ids_ref, mix_ref, sems
):
    tables = [
        pltpu.make_async_copy(source, target, sems.at[index])
        for index, (source, target) in enumerate(((ids_hbm, ids_ref), (mix_hbm, mix_ref)))
    ]
    for table in tables:
        table.start()
    lines, row_count = high_ref.shape
    line = lax.broadcasted_iota(jnp.int32, (lines, row_count), 0)
    expert, part = line // CAP, line % CAP
    parity = expert % CORES
    hit = jnp.zeros((lines, row_count), jnp.float32)
    weight = jnp.zeros((lines, row_count), jnp.float32)
    for table in tables:
        table.wait()
    for pick in range(ids_ref.shape[0]):
        match = ids_ref[pick : pick + 1, :] == expert
        hit = jnp.where(match, 1.0, hit)
        weight = jnp.where(match, mix_ref[pick : pick + 1, :], weight)
    before = lax.broadcasted_iota(jnp.int32, (row_count, row_count), 0)
    after = lax.broadcasted_iota(jnp.int32, (row_count, row_count), 1)
    earlier = jnp.where(before < after, 1.0, 0.0).astype(jnp.bfloat16)
    rank = dot(hit.astype(jnp.bfloat16), earlier)
    combine = jnp.where(rank == part.astype(jnp.float32), weight, 0.0)
    high = combine.astype(jnp.bfloat16)
    high_ref[...] = high
    low_ref[...] = (combine - high.astype(jnp.float32)).astype(jnp.bfloat16)
    slot = jnp.where(parity == 0, slot_ref[0], slot_ref[1]).astype(jnp.float32)
    chosen = jnp.where(rank == slot, hit, 0.0)
    total = dot(jnp.where(part == 0, chosen, 0.0).astype(jnp.bfloat16), own_ref[...])
    theirs = jnp.where(part == 1, chosen, 0.0)
    for core, ref in enumerate((first_ref, second_ref)):
        total = total + dot(jnp.where(parity == core, theirs, 0.0).astype(jnp.bfloat16), ref[...])
    out_ref[...] = total.astype(jnp.bfloat16)


def project_kernel(rows_ref, *refs):
    gates, ups, out_ref, bufs, sems = refs[0:4:2], refs[1:4:2], refs[4], refs[5:7], refs[7]
    copies = [
        pltpu.make_async_copy(source, target, sems.at[index])
        for index, (source, target) in enumerate(zip(ups, bufs))
    ]
    for copy in copies:
        copy.start()
    lines = rows_ref.shape[0]
    hidden = bufs[0].shape[1]
    rows = rows_ref[...]
    parts = [dot(one_hot_rows(lines // CAP, lines, place), rows).astype(jnp.bfloat16) for place in range(CAP)]
    out_ref[:, :hidden] = sum(dot(part, ref[...]) for part, ref in zip(parts, gates)).astype(jnp.bfloat16)
    total = 0.0
    for part, copy, buf in zip(parts, copies, bufs):
        copy.wait()
        total = total + dot(part, buf[...])
    out_ref[:, hidden:] = total.astype(jnp.bfloat16)


def down_kernel(rows_ref, w_ref, out_ref):
    half = rows_ref.shape[0] // CAP
    total = 0.0
    for place in range(CAP):
        result = dot(rows_ref[place * half : (place + 1) * half, :], w_ref[...]).astype(jnp.bfloat16)
        total = total + dot(one_hot_rows(CAP * half, half, place, True), result)
    out_ref[...] = total.astype(jnp.bfloat16)


def combine_kernel(high_ref, low_ref, rows_ref, out_ref):
    rows = rows_ref[...]
    total = 0.0
    for ref in (high_ref, low_ref):
        total = total + lax.dot_general(
            ref[...], rows, (((0,), (0,)), ((), ())), preferred_element_type=jnp.float32
        )
    out_ref[...] = total.astype(jnp.bfloat16)


def run(kernel, shapes, *operands, hbm=(), scratch=(), final=False):
    specs, placed = [], []
    for index, array in enumerate(operands):
        if array.ndim == 1:
            specs.append(pl.BlockSpec(memory_space=pltpu.SMEM))
        elif index in hbm:
            specs.append(pl.BlockSpec(memory_space=pltpu.HBM))
            array = pltpu.with_memory_space_constraint(array, pltpu.HBM)
        else:
            specs.append(pl.BlockSpec(memory_space=pltpu.VMEM))
            array = pltpu.with_memory_space_constraint(array, pltpu.VMEM)
        placed.append(array)
    outs = [
        jax.ShapeDtypeStruct(shape, jnp.bfloat16) if final else pltpu.VMEM(shape, jnp.bfloat16)
        for shape in shapes
    ]
    result = pl.pallas_call(
        kernel,
        in_specs=specs,
        out_specs=[pl.BlockSpec(memory_space=pltpu.VMEM)] * len(outs),
        out_shape=outs,
        scratch_shapes=list(scratch),
        compiler_params=pltpu.CompilerParams(vmem_limit_bytes=16 << 20),
    )(*placed)
    return result if len(outs) > 1 else result[0]


def body(tokens, node_ids, mix_weights, w_gate, w_up, w_down):
    row_count, feat_width = tokens.shape
    node_count = lax.axis_size("node")
    local_count = lax.axis_size("local")
    hidden = w_gate.shape[2]
    members = len(TEAMS[0])
    share = node_count // members

    nodes, places = range(node_count), range(local_count)

    def seat(node, label):
        return node * local_count + (label + node % CORES) % local_count

    def mate(place, core):
        return ((place - core) % local_count ^ 1) + core

    team_groups = [[seat(node, label) for label in team] for node in nodes for team in TEAMS]
    ring_groups = [[seat(node, label) for team in TEAMS for label in team] for node in nodes]
    pair_swap = [(seat(node, label), seat(node, label ^ 1)) for node in nodes for label in places]
    place = lax.axis_index("local")
    slot_of = [
        sum(jnp.where(place == (label + core) % local_count, team, 0) for label, team in enumerate(TEAM))
        for core in range(CORES)
    ]

    def exchange(array, axis, groups=None):
        return lax.all_to_all(
            array, axis, split_axis=0, concat_axis=0, tiled=True, axis_index_groups=groups
        )

    gate_pair = lax.ppermute(w_gate[0], BOTH, pair_swap)
    up_pair = lax.ppermute(w_up[0], BOTH, pair_swap)
    tokens_pair = [
        lax.ppermute(tokens, "local", [(p, mate(p, core) % local_count) for p in places])
        for core in range(CORES)
    ]
    lines = CAP * node_count
    meta = jnp.stack(slot_of).astype(jnp.int32)
    outbound, high, low = run(
        route_kernel,
        [(lines, feat_width), (lines, row_count), (lines, row_count)],
        meta,
        node_ids.T,
        mix_weights.T,
        tokens,
        *tokens_pair,
        hbm=(1, 2),
        scratch=[
            pltpu.VMEM(node_ids.shape[::-1], jnp.int32),
            pltpu.VMEM(mix_weights.shape[::-1], jnp.float32),
            pltpu.SemaphoreType.DMA((2,)),
        ],
    )
    inbound = exchange(outbound.reshape(node_count, CAP, feat_width), "node")
    sums = run(
        project_kernel,
        [(node_count, 2 * hidden)],
        inbound.reshape(lines, feat_width),
        w_gate[0],
        w_up[0],
        gate_pair,
        up_pair,
        hbm=(2, 4),
        scratch=[
            pltpu.VMEM((feat_width, hidden), jnp.bfloat16),
            pltpu.VMEM((feat_width, hidden), jnp.bfloat16),
            pltpu.SemaphoreType.DMA((2,)),
        ],
    )
    parts = exchange(sums.reshape(members, share, 2 * hidden), BOTH, team_groups)
    total = jnp.sum(parts.astype(jnp.float32), axis=0)
    active = (jax.nn.silu(total[:, :hidden]) * total[:, hidden:]).astype(jnp.bfloat16)

    copies = jnp.broadcast_to(active[None], (local_count, share, hidden))
    rows = exchange(copies, BOTH, ring_groups).reshape(lines, hidden)
    result = run(down_kernel, [(lines, feat_width)], rows, w_down[0])
    returned = exchange(result.reshape(node_count, CAP, feat_width), "node").reshape(lines, feat_width)
    return run(combine_kernel, [(row_count, feat_width)], high, low, returned, final=True)


def solution(mesh):
    return jax.shard_map(
        body,
        mesh=mesh,
        in_specs=(
            P("node", "local"),
            P("node", None),
            P("node", None),
            P("node", "local", None),
            P("node", "local", None),
            P("node", None, "local"),
        ),
        out_specs=P("node", "local"),
        check_vma=False,
    )
```
